32 devices in a mesh: dp: 8 (over z, core), sp: 4 (over y, x).
Axes of the slice: x: 2, y: 2, z: 4, core: 2. Of those that a mesh axis runs over, the one named last changes fastest.
Arguments:
- gate_pre: bfloat16 [2048, 8192], P('dp', 'sp'), may hold values from -6 to 6
- up_pre: bfloat16 [2048, 8192], P('dp', 'sp'), may hold values from -6 to 6
- w_down: bfloat16 [8192, 6144], P('sp'), may hold values from -0.0625 to 0.0625
- route_logits: float32 [4096, 2], P(('dp', 'sp')), may hold values from -8 to 8
- expert_ids: int32 [4096, 2], P(('dp', 'sp')), may hold values from 0 to 7, as said below
- d_out: bfloat16 [4096, 6144], P(('dp', 'sp')), may hold values from -6 to 6
Outputs:
- mixed: bfloat16 [4096, 6144], P(('dp', 'sp'))
- logit_grads: float32 [4096, 2], P(('dp', 'sp'))
- gate_grads: bfloat16 [2048, 8192], P('dp', 'sp')
- up_grads: bfloat16 [2048, 8192], P('dp', 'sp')
- down_grads: float32 [8192, 6144], P('sp', 'dp')
The draws below stay inside these ranges and needn't reach their ends.
Inputs may be any that keep to these rules, and one draw needn't show every extreme that they name: `expert_ids`: each row names two different experts. Of the 128 rows of one device, a quarter of 64 up to 64 name expert 0, and exactly 64 on some device in every draw.
All inputs are finite; a program needn't handle non-finite values.
Results may differ from the reference program's by a relative error of at most 0.022.
Values may be sent and summed in bfloat16 or wider, within the bound.
A program may use at most 128 MiB of HBM per device.

```python
import jax
import jax.numpy as jnp
from jax import lax

D = 6144
TOPK = 2
HID = 8192
TOK_DEV = 128
SLOT_DEV = 64
SLOTS = 256
TOKENS = 4096
N_DP = 8
N_SP = 4


def draw_expert_ids(key, part):
    blocks_all = TOKENS // TOK_DEV
    key_count = jax.random.fold_in(key, 11)
    key_full = jax.random.fold_in(key, 12)
    key_order = jax.random.fold_in(key, 13)
    key_other = jax.random.fold_in(key, 14)
    key_first = jax.random.fold_in(key, 15)
    key_step = jax.random.fold_in(key, 16)
    key_swap = jax.random.fold_in(key, 17)
    loads = jax.random.randint(key_count, (blocks_all,), SLOT_DEV // 4, SLOT_DEV + 1)
    full_block = jax.random.randint(key_full, (), 0, blocks_all)
    loads = jnp.where(jnp.arange(blocks_all) == full_block, SLOT_DEV, loads)
    order_keys = jax.random.split(key_order, blocks_all)
    ranks = jax.vmap(lambda one_key: jax.random.permutation(one_key, TOK_DEV))(order_keys)
    chosen = (ranks < loads[:, None]).reshape(TOKENS)
    other = jax.random.randint(key_other, (TOKENS,), 1, 8)
    first = jax.random.randint(key_first, (TOKENS,), 1, 8)
    second = 1 + (first - 1 + jax.random.randint(key_step, (TOKENS,), 1, 7)) % 7
    column_a = jnp.where(chosen, 0, first)
    column_b = jnp.where(chosen, other, second)
    swapped = jax.random.randint(key_swap, (TOKENS,), 0, 2) == 1
    left = jnp.where(swapped, column_b, column_a)
    right = jnp.where(swapped, column_a, column_b)
    return jnp.stack([left, right], axis=1).astype(jnp.int32)


def raised(entries, stream_key, source, target, parts, factor):
    def block_of(position):
        return (jnp.arange(entries.shape[position]) // (entries.shape[position] // parts)).reshape((-1,) + (1,) * (entries.ndim - 1 - position))

    one_side = jax.random.permutation(stream_key, parts)[block_of(target)]
    other_side = (block_of(target) + parts // 2) % parts
    return jnp.where((block_of(source) == one_side) | (block_of(source) == other_side), factor * entries, entries)


def steps_of(key, extent, shards, low, high):
    gain, own = 1.0, jax.random.fold_in(key, 6)
    for dim, blocks in shards:
        steps = jnp.exp(jax.random.uniform(jax.random.fold_in(own, dim), (blocks,), jnp.float32, low / len(shards), high / len(shards)))
        gain = gain * jnp.repeat(steps, extent[dim] // blocks).reshape([-1 if axis == dim else 1 for axis in range(len(extent))])
    return gain


def scatter_about(own_key, shape, spread, bound, pieces=(), held_as=jnp.bfloat16):
    entries = spread * jax.random.normal(own_key, shape, jnp.float32)
    if pieces:
        entries = entries * steps_of(own_key, shape, pieces, -0.22, 0.18)
    return jnp.clip(entries, -bound, bound).astype(held_as)


def heavy_noise(rng, dims, deviation, bound, shards, heavy, held_as=jnp.bfloat16):
    entries = deviation * jax.random.normal(rng, dims, jnp.float32)
    if shards:
        entries = entries * steps_of(rng, dims, shards, -0.22, 0.18)
    return jnp.clip(raised(entries, jax.random.fold_in(rng, 3), *heavy), -bound, bound).astype(held_as)


def setup_inputs(seed: int = 0) -> dict:
    seeds = jax.random.split(jax.random.key(seed), 7)
    return {
        "gate_pre": scatter_about(seeds[0], (SLOTS * N_DP, HID), 1.0, 6.0, ((0, 8), (1, 4))),
        "up_pre": scatter_about(seeds[1], (SLOTS * N_DP, HID), 1.0, 6.0, ((0, 8), (1, 4))),
        "w_down": scatter_about(seeds[2], (HID, D), HID ** -0.5, 0.0625, ((0, 4),)),
        "route_logits": scatter_about(seeds[3], (TOKENS, TOPK), 2.0, 8.0, ((0, 32),), jnp.float32),
        "expert_ids": draw_expert_ids(jax.random.fold_in(seeds[6], 71), 0),
        "d_out": heavy_noise(seeds[5], (TOKENS, D), 1.0, 6.0, ((0, 32),), (0, 1, 32, 2.75)),
    }


def reference(gate_pre, up_pre, w_down, route_logits, expert_ids, d_out):
    cycle_tokens = TOK_DEV * N_SP
    local_width = HID // N_SP

    def cycle_pass(grad_total, inputs):
        gate_cycle, up_cycle, logit_cycle, expert_cycle, cot_cycle = inputs
        gate_wide = gate_cycle.astype(jnp.float32)
        up_wide = up_cycle.astype(jnp.float32)
        sigma_gate = jax.nn.sigmoid(gate_wide)
        silu_gate = gate_wide * sigma_gate
        hidden = (silu_gate * up_wide).astype(jnp.bfloat16)
        routed = jnp.any(expert_cycle == 0, axis=1)
        routed_int = routed.astype(jnp.int32)
        slot_rank = (jnp.cumsum(routed_int.reshape(N_SP, TOK_DEV), axis=1) - 1).reshape(cycle_tokens).astype(jnp.int32)
        owner = jnp.arange(cycle_tokens, dtype=jnp.int32) // TOK_DEV
        slot_index = (owner * SLOT_DEV + slot_rank).astype(jnp.int32)
        expert_out = jnp.zeros((SLOTS, D), jnp.float32)
        for member in range(N_SP):
            lower = member * local_width
            partial_out = jnp.dot(hidden[:, lower:lower + local_width], w_down[lower:lower + local_width], preferred_element_type=jnp.float32)
            expert_out = expert_out + lax.optimization_barrier(partial_out.astype(jnp.bfloat16)).astype(jnp.float32)
        routed_float = routed.astype(jnp.float32)
        token_out = expert_out[jnp.where(routed, slot_index, 0)] * routed_float[:, None]
        first_zero = expert_cycle[:, 0] == 0
        own_logit = jnp.where(first_zero, logit_cycle[:, 0], logit_cycle[:, 1])
        other_logit = jnp.where(first_zero, logit_cycle[:, 1], logit_cycle[:, 0])
        weight_zero = routed_float * jax.nn.sigmoid(own_logit - other_logit)
        mixed = (weight_zero[:, None] * token_out).astype(jnp.bfloat16)
        weight_grad = jnp.sum(cot_cycle.astype(jnp.float32) * token_out, axis=1)
        logit_grad = weight_grad * weight_zero * (1.0 - weight_zero)
        first_col = jnp.where(first_zero, logit_grad, -logit_grad)
        logit_grads = jnp.stack([first_col, -first_col], axis=1)
        slot_cot = (weight_zero[:, None] * cot_cycle.astype(jnp.float32)).astype(jnp.bfloat16)
        target = jnp.where(routed, slot_index, SLOTS).astype(jnp.int32)
        d_expert = jnp.zeros((SLOTS, D), jnp.bfloat16).at[target].set(slot_cot, mode="drop")
        d_hidden = jnp.dot(d_expert, w_down.T, preferred_element_type=jnp.float32)
        gate_grads = (d_hidden * up_wide * sigma_gate * (1.0 + gate_wide * (1.0 - sigma_gate))).astype(jnp.bfloat16)
        up_grads = (d_hidden * silu_gate).astype(jnp.bfloat16)
        grad_total = grad_total + jnp.dot(hidden.T, d_expert, preferred_element_type=jnp.float32)
        return grad_total, (mixed, logit_grads, gate_grads, up_grads)

    inputs = (gate_pre.reshape(N_DP, SLOTS, HID), up_pre.reshape(N_DP, SLOTS, HID),
              route_logits.reshape(N_DP, cycle_tokens, TOPK), expert_ids.reshape(N_DP, cycle_tokens, TOPK),
              d_out.reshape(N_DP, cycle_tokens, D))
    down_grads, stacked = lax.scan(cycle_pass, jnp.zeros((HID, D), jnp.float32), inputs)
    mixed, logit_grads, gate_grads, up_grads = stacked
    return (mixed.reshape(TOKENS, D), logit_grads.reshape(TOKENS, TOPK),
            gate_grads.reshape(SLOTS * N_DP, HID), up_grads.reshape(SLOTS * N_DP, HID), down_grads)
```

```python
import functools
import math

import jax
import jax.numpy as jnp
from jax import lax
from jax.experimental import pallas as pl
from jax.experimental.pallas import tpu as pltpu
from jax.sharding import PartitionSpec as P

MESH = pl.DeviceIdType.MESH
PIECES = 4


def fused_kernel(
    n_dp, n_sp, ids_ref, logit_ref, gate_hbm, up_hbm, w_ref, dout_hbm,
    mixed_ref, lgrad_ref, ggrad_ref, ugrad_ref, down_ref,
    gate, up, dout, hall, dall, dcyc, part, rs_ref, wcol, wrow,
    choose_slot, slot_weight, choose_tok, token_weight, wgrad,
    load_sem, wsem, local_sem, right_send, left_send, pair_send, hrecv, asend, arecv,
    gsend, grecv, bsend, brecv, rsend, rrecv, fsend, frecv, mate_send,
):
    f32, bf = jnp.float32, jnp.bfloat16
    dp, sp = lax.axis_index("dp"), lax.axis_index("sp")
    chips = n_dp // 2
    chip, core = lax.div(dp, 2), lax.rem(dp, 2)
    partner = chip * 2 + 1 - core
    slots, hid_width = gate.shape
    tokens, width = dout.shape
    slot_rows = dcyc.shape[1]
    block = width // n_dp
    rows = slots // PIECES
    tn = wcol.shape[2]
    th = wrow.shape[1]
    n_col, n_row = width // tn, hid_width // th

    barrier = pltpu.get_barrier_semaphore()
    for off in range(1, n_dp):
        pl.semaphore_signal(barrier, inc=1, device_id={"dp": lax.rem(dp + off, n_dp)}, device_id_type=MESH)
    for off in range(1, n_sp):
        pl.semaphore_signal(barrier, inc=1, device_id={"sp": lax.rem(sp + off, n_sp)}, device_id_type=MESH)

    def piece_rows(p):
        return slice(p * rows, (p + 1) * rows)

    def gate_load(p):
        return pltpu.make_async_copy(gate_hbm.at[piece_rows(p)], gate.at[piece_rows(p)], load_sem.at[2 * p])

    def up_load(p):
        return pltpu.make_async_copy(up_hbm.at[piece_rows(p)], up.at[piece_rows(p)], load_sem.at[2 * p + 1])

    dout_load = pltpu.make_async_copy(dout_hbm, dout, load_sem.at[2 * PIECES])

    def col_load(step, slot):
        return pltpu.make_async_copy(
            w_ref.at[:, pl.ds(pl.multiple_of(step * tn, tn), tn)], wcol.at[slot], wsem.at[slot]
        )

    def row_load(step, slot):
        return pltpu.make_async_copy(
            w_ref.at[pl.ds(pl.multiple_of(step * th, th), th), :], wrow.at[slot], wsem.at[2 + slot]
        )

    gate_load(0).start()
    up_load(0).start()
    dout_load.start()
    for p in range(1, PIECES):
        gate_load(p).start()
        up_load(p).start()
    col_load(0, 0).start()
    row_load(0, 0).start()

    def remote(src, dst, send, recv, **where):
        return pltpu.make_async_remote_copy(
            src_ref=src, dst_ref=dst, send_sem=send, recv_sem=recv, device_id=where, device_id_type=MESH
        )

    def arrived(ref, sem):
        pltpu.make_async_copy(ref, ref, sem).wait()

    def block_cols(index):
        return pl.ds(pl.multiple_of(index * block, block), block)

    zero = (ids_ref[...] == 0).astype(f32)
    first, second = zero[0:1, :], zero[1:2, :]
    routed = jnp.maximum(first, second)
    logits = logit_ref[...]
    own_logit = jnp.where(first > 0.0, logits[0:1, :], logits[1:2, :])
    other_logit = jnp.where(first > 0.0, logits[1:2, :], logits[0:1, :])
    weight = routed * jax.nn.sigmoid(own_logit - other_logit)
    along = lax.broadcasted_iota(jnp.int32, (tokens, tokens), 0)
    across = lax.broadcasted_iota(jnp.int32, (tokens, tokens), 1)
    before = jnp.where(along <= across, 1.0, 0.0).astype(bf)
    rank = jnp.dot(jnp.broadcast_to(routed, (16, tokens)).astype(bf), before, preferred_element_type=f32)[0:1, :] - 1.0
    chooser = jnp.where(along.astype(f32) == rank, 1.0, 0.0) * routed
    choose_slot[...] = chooser[:slot_rows, :].astype(bf)
    slot_weight[...] = jnp.sum(chooser[:slot_rows, :] * weight, axis=1, keepdims=True)
    choose_tok[...] = jnp.transpose(chooser).astype(bf)
    token_weight[...] = jnp.transpose(jnp.broadcast_to(weight, (tokens, tokens)))

    def make_hidden(p):
        gate_load(p).wait()
        up_load(p).wait()

        def step(i, carry):
            here = pl.ds(pl.multiple_of(p * rows + i * 16, 16), 16)
            gate_wide = gate[here, :].astype(f32)
            silu = gate_wide * jax.nn.sigmoid(gate_wide)
            hall[dp, here, :] = (silu * up[here, :].astype(f32)).astype(bf)
            return carry

        lax.fori_loop(0, rows // 16, step, 0)

    def piece(index, p):
        return hall.at[index, piece_rows(p)]

    def h_send(index, p, to, send):
        return remote(piece(index, p), piece(index, p), send, hrecv.at[PIECES * index + p], dp=to)

    def h_wait(index, p):
        arrived(piece(index, p), hrecv.at[PIECES * index + p])

    def h_right(index, p, step):
        return h_send(index, p, dp + 2, right_send.at[PIECES * step + p])

    def h_left(index, p, step):
        return h_send(index, p, dp - 2, left_send.at[PIECES * step + p])

    def h_pair(index, p):
        return h_send(index, p, partner, pair_send.at[PIECES * lax.div(index, 2) + p])

    def send_own(p):
        @pl.when(chip + 1 < chips)
        def _():
            h_right(dp, p, 0).start()

        @pl.when(chip >= 1)
        def _():
            h_left(dp, p, 0).start()

        h_pair(dp, p).start()

    def a_send(apart, to_core):
        other = 2 * lax.rem(chip + apart, chips) + to_core
        return remote(
            dcyc.at[sp, :, block_cols(other)], dall.at[2 * (chips - apart) + core, sp],
            asend.at[2 * apart + to_core], arecv.at[2 * (chips - apart) + core], dp=other,
        )

    away = [(apart, to_core) for apart in range(1, chips) for to_core in range(2)]

    make_hidden(0)
    pl.semaphore_wait(barrier, n_dp - 1 + n_sp - 1)
    send_own(0)

    dout_load.wait()

    def slot_step(step, carry):
        cols = pl.ds(pl.multiple_of(step * tn, tn), tn)
        picked = jnp.dot(choose_slot[...], dout[:, cols], preferred_element_type=f32)
        dcyc[sp, :, cols] = (slot_weight[...] * picked).astype(bf)
        return carry

    lax.fori_loop(0, n_col, slot_step, 0)

    relayed = n_sp == 4
    if relayed:
        near = [sp + 1 - 2 * lax.rem(sp, 2), lax.rem(sp + 2, 4)]
    else:
        near = [lax.rem(sp + off, n_sp) for off in range(1, n_sp)]
    ways = range(len(near))
    half_rows, half_dp = slot_rows // 2, (n_dp - 2) // 2

    def g_send(way):
        return remote(dcyc.at[sp], dcyc.at[sp], gsend.at[way], grecv.at[sp], sp=near[way])

    def b_send(way):
        return remote(dall.at[2:, sp], dall.at[2:, sp], bsend.at[way], brecv.at[sp], sp=near[way])

    def g_half(source, way):
        return dcyc.at[source, way * half_rows:(way + 1) * half_rows]

    def b_half(source, way):
        return dall.at[2 + way * half_dp:2 + (way + 1) * half_dp, source]

    def g_pass(way):
        held = g_half(near[way], way)
        return remote(held, held, fsend.at[way], frecv.at[way], sp=near[1 - way])

    def b_pass(way):
        held = b_half(near[way], way)
        return remote(held, held, fsend.at[2 + way], frecv.at[2 + way], sp=near[1 - way])

    for way in ways:
        g_send(way).start()
    for p in range(1, PIECES):
        make_hidden(p)
        send_own(p)
    for apart, to_core in away:
        a_send(apart, to_core).start()

    def r_send(step, off):
        other = lax.rem(sp + off, n_sp)
        cols = pl.ds(pl.multiple_of(step * tn, tn), tn)
        return remote(
            part.at[other, :, cols], rs_ref.at[sp, :, cols],
            rsend.at[step, off], rrecv.at[step, sp], sp=other,
        )

    def half_cols(step, way):
        half = tn // 2
        return pl.ds(pl.multiple_of(step * tn + way * half, half), half)

    def r_hop(step, way, kind):
        cols = half_cols(step, way)
        src = [part.at[near[way], :, cols], part.at[3 - sp, :, cols], rs_ref.at[3, :, cols]][kind]
        return remote(
            src, rs_ref.at[kind, :, cols], rsend.at[step, 2 * kind + way], rrecv.at[step, 2 * kind + way],
            sp=near[1 - way if kind == 2 else way],
        )

    def r_arrived(step, way, kind):
        arrived(rs_ref.at[kind, :, half_cols(step, way)], rrecv.at[step, 2 * kind + way])

    def fold_step(step, carry):
        for way in range(2):
            cols = half_cols(step, way)
            r_arrived(step, way, 1)
            rs_ref[3, :, cols] = (
                part[near[1 - way], :, cols].astype(f32) + rs_ref[1, :, cols].astype(f32)
            ).astype(bf)
            r_hop(step, way, 2).start()
        return carry

    def col_step(step, carry):
        slot = lax.rem(step, 2)

        @pl.when(step + 1 < n_col)
        def _():
            col_load(step + 1, 1 - slot).start()

        col_load(step, slot).wait()
        cols = pl.ds(pl.multiple_of(step * tn, tn), tn)
        product = jnp.dot(hall[dp], wcol[slot], preferred_element_type=f32)
        part[:, :, cols] = product.astype(bf).reshape(n_sp, slot_rows, tn)
        if relayed:
            for kind in (1, 0):
                for way in range(2):
                    r_hop(step, way, kind).start()
        else:
            for off in range(1, n_sp):
                r_send(step, off).start()
        return carry

    lax.fori_loop(0, n_col, col_step, 0)

    def relay(step, p):
        @pl.when(chip - step >= 0)
        def _():
            index = dp - 2 * step
            h_wait(index, p)

            @pl.when(chip + 1 < chips)
            def _():
                h_right(index, p, step).start()

            h_pair(index, p).start()

        @pl.when(chip + step < chips)
        def _():
            index = dp + 2 * step
            h_wait(index, p)

            @pl.when(chip >= 1)
            def _():
                h_left(index, p, step).start()

            h_pair(index, p).start()

    last = chips - 1
    for p in range(PIECES - 1):
        if last > 1:
            relay(1, p)
    for way in ways:
        arrived(dcyc.at[near[way]], grecv.at[near[way]])
        if relayed:
            g_pass(way).start()
    if last > 1:
        relay(1, PIECES - 1)

    if relayed:
        lax.fori_loop(0, n_col, fold_step, 0)

    for slot in range(2, n_dp):
        arrived(dall.at[slot, sp], arecv.at[slot])
    for way in ways:
        b_send(way).start()

    if relayed:
        for way in ways:
            arrived(g_half(3 - sp, way), frecv.at[way])

    own_copy = pltpu.make_async_copy(dcyc.at[:, :, block_cols(dp)], dall.at[core], local_sem.at[0])
    mate_copy = remote(
        dcyc.at[:, :, block_cols(partner)], dall.at[core], mate_send.at[0], arecv.at[core], dp=partner
    )
    own_copy.start()
    mate_copy.start()

    def row_step(step, carry):
        slot = lax.rem(step, 2)

        @pl.when(step + 1 < n_row)
        def _():
            row_load(step + 1, 1 - slot).start()

        row_load(step, slot).wait()
        cols = pl.ds(pl.multiple_of(step * th, th), th)
        d_hidden = lax.dot_general(
            dcyc[...].reshape(slots, width), wrow[slot], (((1,), (1,)), ((), ())), preferred_element_type=f32
        )
        gate_wide, up_wide = gate[:, cols].astype(f32), up[:, cols].astype(f32)
        sigma = jax.nn.sigmoid(gate_wide)
        ggrad_ref[:, cols] = (d_hidden * up_wide * sigma * (1.0 + gate_wide * (1.0 - sigma))).astype(bf)
        ugrad_ref[:, cols] = (d_hidden * (gate_wide * sigma)).astype(bf)
        return carry

    for p in range(PIECES):
        lax.fori_loop(p * n_row // PIECES, (p + 1) * n_row // PIECES, row_step, 0)
        if last > 2:
            relay(2, p)

    tw = min(256, hid_width)
    half_slots, half_sp = slots // 2, n_sp // 2

    def down_pass(source, half, initial):
        rel = lax.rem(source - chip + chips, chips)
        span, here, owners = slots, slice(None), slice(None)
        if half is not None:
            span = half_slots
            here, owners = slice(half * half_slots, (half + 1) * half_slots), slice(half * half_sp, (half + 1) * half_sp)

        def step(i, carry):
            cols = pl.ds(pl.multiple_of(i * tw, tw), tw)
            product = lax.dot_general(
                hall[pl.ds(2 * source, 2), here, cols].reshape(2 * span, tw),
                dall[pl.ds(2 * rel, 2), owners].reshape(2 * span, block),
                (((0,), (0,)), ((), ())), preferred_element_type=f32,
            )
            if initial:
                down_ref[cols, :] = product
            else:
                down_ref[cols, :] += product
            return carry

        lax.fori_loop(0, hid_width // tw, step, 0)

    own_copy.wait()
    arrived(dall.at[1 - core], arecv.at[1 - core])
    for p in range(PIECES):
        h_wait(partner, p)
    down_pass(chip, None, True)

    wgrad[...] = jnp.zeros_like(wgrad)

    def mix_step(step, carry):
        cols = pl.ds(pl.multiple_of(step * tn, tn), tn)
        total = part[sp, :, cols].astype(f32)
        if relayed:
            for kind in (0, 2):
                for way in range(2):
                    r_arrived(step, way, kind)
                total = total + rs_ref[kind, :, cols].astype(f32)
        else:
            for off in range(1, n_sp):
                other = lax.rem(sp + off, n_sp)
                arrived(rs_ref.at[other, :, cols], rrecv.at[step, other])
                total = total + rs_ref[other, :, cols].astype(f32)
        high = total.astype(bf)
        low = (total - high.astype(f32)).astype(bf)
        choose = choose_tok[:, :slot_rows]
        token_out = jnp.dot(choose, high, preferred_element_type=f32) + jnp.dot(
            choose, low, preferred_element_type=f32
        )
        mixed_ref[:, cols] = (token_weight[:, 0:1] * token_out).astype(bf)
        wgrad[...] += jnp.sum(dout[:, cols].astype(f32) * token_out, axis=1, keepdims=True)
        if relayed:
            for kind in range(3):
                for way in range(2):
                    r_hop(step, way, kind).wait_send()
        else:
            for off in range(1, n_sp):
                r_send(step, off).wait_send()
        return carry

    lax.fori_loop(0, n_col, mix_step, 0)

    slope = jnp.transpose(jnp.broadcast_to(wgrad[...], (tokens, tokens)))[0:1, :] * weight * (1.0 - weight)
    first_col = jnp.where(first > 0.0, slope, -slope)
    lgrad_ref[0:1, :] = first_col
    lgrad_ref[1:2, :] = -first_col

    for way in ways:
        arrived(dall.at[2:, near[way]], brecv.at[near[way]])
        if relayed:
            b_pass(way).start()

    for step in range(3, last):
        for p in range(PIECES):
            relay(step, p)

    if relayed:
        for way in ways:
            arrived(b_half(3 - sp, way), frecv.at[2 + way])

    def down_step(index, carry):
        source = chip + (lax.div(index, 2) + 1) * (2 * lax.rem(index, 2) - 1)

        @pl.when((source >= 0) & (source < chips))
        def _():
            for p in range(PIECES):
                h_wait(2 * source + 1 - core, p)
            down_pass(source, None, False)

        return carry

    if last > 1:
        lax.fori_loop(0, 2 * (last - 1), down_step, 0)

    if last > 0:
        @pl.when((chip == 0) | (chip == last))
        def _():
            source = last - chip
            for half in range(2):
                mine = range(half * PIECES // 2, (half + 1) * PIECES // 2)
                for p in mine:
                    h_wait(2 * source + core, p)
                    h_pair(2 * source + core, p).start()
                for p in mine:
                    h_wait(2 * source + 1 - core, p)
                down_pass(source, half, False)

    mate_copy.wait_send()
    for way in ways:
        g_send(way).wait_send()
        b_send(way).wait_send()
        if relayed:
            g_pass(way).wait_send()
            b_pass(way).wait_send()
    for apart, to_core in away:
        a_send(apart, to_core).wait_send()
    for step in range(chips):
        for p in range(PIECES):
            @pl.when((chip - step >= 0) & (chip + 1 < chips))
            def _():
                h_right(dp, p, step).wait_send()

            @pl.when((chip + step < chips) & (chip >= 1))
            def _():
                h_left(dp, p, step).wait_send()

            h_send(dp, p, partner, pair_send.at[PIECES * step + p]).wait_send()


def fused(n_dp, n_sp, ids, logits, gate_pre, up_pre, w_down, d_out):
    slots, hid_width = gate_pre.shape
    tokens, width = d_out.shape
    slot_rows = slots // n_sp
    block = width // n_dp
    tn, th = width // 8, min(256, hid_width)
    n_col = width // tn
    chips = n_dp // 2
    f32, bf = jnp.float32, jnp.bfloat16
    dma = pltpu.SemaphoreType.DMA
    hbm = pl.BlockSpec(memory_space=pl.ANY)
    vmem = pl.BlockSpec(memory_space=pltpu.VMEM)
    buffers = [
        ((slots, hid_width), bf), ((slots, hid_width), bf), ((tokens, width), bf),
        ((n_dp, slots, hid_width), bf), ((n_dp, n_sp, slot_rows, block), bf),
        ((n_sp, slot_rows, width), bf), ((n_sp, slot_rows, width), bf), ((n_sp, slot_rows, width), bf),
        ((2, hid_width, tn), bf), ((2, th, width), bf),
        ((slot_rows, tokens), bf), ((slot_rows, 1), f32), ((tokens, tokens), bf), ((tokens, tokens), f32),
        ((tokens, 1), f32),
    ]
    held = sum(math.prod(shape) * jnp.dtype(dtype).itemsize for shape, dtype in buffers)
    return pl.pallas_call(
        functools.partial(fused_kernel, n_dp, n_sp),
        out_shape=(
            pltpu.VMEM((tokens, width), bf),
            pltpu.VMEM((2, tokens), f32),
            pltpu.VMEM((slots, hid_width), bf),
            pltpu.VMEM((slots, hid_width), bf),
            pltpu.VMEM((hid_width, block), f32),
        ),
        in_specs=[vmem, vmem, hbm, hbm, hbm, hbm],
        out_specs=(vmem,) * 5,
        scratch_shapes=[pltpu.VMEM(shape, dtype) for shape, dtype in buffers] + [
            dma((2 * PIECES + 1,)),
            dma((4,)),
            dma((1,)),
            dma((PIECES * chips,)),
            dma((PIECES * chips,)),
            dma((PIECES * chips,)),
            dma((PIECES * n_dp,)),
            dma((n_dp,)),
            dma((n_dp,)),
            dma((n_sp,)),
            dma((n_sp,)),
            dma((n_sp,)),
            dma((n_sp,)),
            dma((n_col, max(n_sp, 6))),
            dma((n_col, max(n_sp, 6))),
            dma((4,)),
            dma((4,)),
            dma((1,)),
        ],
        compiler_params=pltpu.CompilerParams(
            collective_id=0, has_side_effects=True, vmem_limit_bytes=held + 4 * 1024 * 1024
        ),
    )(ids, logits, gate_pre, up_pre, w_down, d_out)


def local(n_dp, n_sp, gate_pre, up_pre, w_down, route_logits, expert_ids, d_out):
    mixed, slopes, gate_grads, up_grads, down_grads = fused(
        n_dp, n_sp, expert_ids.T, route_logits.T, gate_pre, up_pre, w_down, d_out
    )
    return (mixed, slopes.T, gate_grads, up_grads, down_grads)


def solution(mesh):
    both = P(("dp", "sp"), None)
    return jax.shard_map(
        functools.partial(local, mesh.shape["dp"], mesh.shape["sp"]),
        mesh=mesh,
        in_specs=(P("dp", "sp"), P("dp", "sp"), P("sp", None), both, both, both),
        out_specs=(both, both, P("dp", "sp"), P("dp", "sp"), P("sp", "dp")),
        check_vma=False,
    )
```

```python
import functools
import math

import jax
import jax.numpy as jnp
from jax import lax
from jax.experimental import pallas as pl
from jax.experimental.pallas import tpu as pltpu
from jax.sharding import PartitionSpec as P

MESH = pl.DeviceIdType.MESH
PIECES = 4


def fused_kernel(
    n_dp, n_sp, ids_ref, logit_ref, gate_hbm, up_hbm, w_ref, dout_hbm,
    mixed_ref, lgrad_ref, ggrad_ref, ugrad_ref, down_ref,
    gate, up, dout, hall, dall, dcyc, part, rs_ref, wcol, wrow,
    choose_slot, slot_weight, choose_tok, token_weight, wgrad,
    load_sem, wsem, local_sem, right_send, left_send, pair_send, hrecv, asend, arecv,
    gsend, grecv, bsend, brecv, rsend, rrecv, fsend, frecv, mate_send,
):
    f32, bf = jnp.float32, jnp.bfloat16
    dp, sp = lax.axis_index("dp"), lax.axis_index("sp")
    chips = n_dp // 2
    chip, core = lax.div(dp, 2), lax.rem(dp, 2)
    partner = chip * 2 + 1 - core
    slots, hid_width = gate.shape
    tokens, width = dout.shape
    slot_rows = dcyc.shape[1]
    block = width // n_dp
    rows = slots // PIECES
    tn = wcol.shape[2]
    th = wrow.shape[1]
    n_col, n_row = width // tn, hid_width // th

    barrier = pltpu.get_barrier_semaphore()
    for off in range(1, n_dp):
        pl.semaphore_signal(barrier, inc=1, device_id={"dp": lax.rem(dp + off, n_dp)}, device_id_type=MESH)
    for off in range(1, n_sp):
        pl.semaphore_signal(barrier, inc=1, device_id={"sp": lax.rem(sp + off, n_sp)}, device_id_type=MESH)

    def piece_rows(p):
        return slice(p * rows, (p + 1) * rows)

    def gate_load(p):
        return pltpu.make_async_copy(gate_hbm.at[piece_rows(p)], gate.at[piece_rows(p)], load_sem.at[2 * p])

    def up_load(p):
        return pltpu.make_async_copy(up_hbm.at[piece_rows(p)], up.at[piece_rows(p)], load_sem.at[2 * p + 1])

    dout_load = pltpu.make_async_copy(dout_hbm, dout, load_sem.at[2 * PIECES])

    def col_load(step, slot):
        return pltpu.make_async_copy(
            w_ref.at[:, pl.ds(pl.multiple_of(step * tn, tn), tn)], wcol.at[slot], wsem.at[slot]
        )

    def row_load(step, slot):
        return pltpu.make_async_copy(
            w_ref.at[pl.ds(pl.multiple_of(step * th, th), th), :], wrow.at[slot], wsem.at[2 + slot]
        )

    gate_load(0).start()
    up_load(0).start()
    dout_load.start()
    for p in range(1, PIECES):
        gate_load(p).start()
        up_load(p).start()
    col_load(0, 0).start()
    row_load(0, 0).start()

    def remote(src, dst, send, recv, **where):
        return pltpu.make_async_remote_copy(
            src_ref=src, dst_ref=dst, send_sem=send, recv_sem=recv, device_id=where, device_id_type=MESH
        )

    def arrived(ref, sem):
        pltpu.make_async_copy(ref, ref, sem).wait()

    def block_cols(index):
        return pl.ds(pl.multiple_of(index * block, block), block)

    zero = (ids_ref[...] == 0).astype(f32)
    first, second = zero[0:1, :], zero[1:2, :]
    routed = jnp.maximum(first, second)
    logits = logit_ref[...]
    own_logit = jnp.where(first > 0.0, logits[0:1, :], logits[1:2, :])
    other_logit = jnp.where(first > 0.0, logits[1:2, :], logits[0:1, :])
    weight = routed * jax.nn.sigmoid(own_logit - other_logit)
    along = lax.broadcasted_iota(jnp.int32, (tokens, tokens), 0)
    across = lax.broadcasted_iota(jnp.int32, (tokens, tokens), 1)
    before = jnp.where(along <= across, 1.0, 0.0).astype(bf)
    rank = jnp.dot(jnp.broadcast_to(routed, (16, tokens)).astype(bf), before, preferred_element_type=f32)[0:1, :] - 1.0
    chooser = jnp.where(along.astype(f32) == rank, 1.0, 0.0) * routed
    choose_slot[...] = chooser[:slot_rows, :].astype(bf)
    slot_weight[...] = jnp.sum(chooser[:slot_rows, :] * weight, axis=1, keepdims=True)
    choose_tok[...] = jnp.transpose(chooser).astype(bf)
    token_weight[...] = jnp.transpose(jnp.broadcast_to(weight, (tokens, tokens)))

    def make_hidden(p):
        gate_load(p).wait()
        up_load(p).wait()

        def step(i, carry):
            here = pl.ds(pl.multiple_of(p * rows + i * 16, 16), 16)
            gate_wide = gate[here, :].astype(f32)
            silu = gate_wide * jax.nn.sigmoid(gate_wide)
            hall[dp, here, :] = (silu * up[here, :].astype(f32)).astype(bf)
            return carry

        lax.fori_loop(0, rows // 16, step, 0)

    def piece(index, p):
        return hall.at[index, piece_rows(p)]

    def h_send(index, p, to, send):
        return remote(piece(index, p), piece(index, p), send, hrecv.at[PIECES * index + p], dp=to)

    def h_wait(index, p):
        arrived(piece(index, p), hrecv.at[PIECES * index + p])

    def h_right(index, p, step):
        return h_send(index, p, dp + 2, right_send.at[PIECES * step + p])

    def h_left(index, p, step):
        return h_send(index, p, dp - 2, left_send.at[PIECES * step + p])

    def h_pair(index, p):
        return h_send(index, p, partner, pair_send.at[PIECES * lax.div(index, 2) + p])

    def send_own(p):
        @pl.when(chip + 1 < chips)
        def _():
            h_right(dp, p, 0).start()

        @pl.when(chip >= 1)
        def _():
            h_left(dp, p, 0).start()

        h_pair(dp, p).start()

    def a_send(apart, to_core):
        other = 2 * lax.rem(chip + apart, chips) + to_core
        return remote(
            dcyc.at[sp, :, block_cols(other)], dall.at[2 * (chips - apart) + core, sp],
            asend.at[2 * apart + to_core], arecv.at[2 * (chips - apart) + core], dp=other,
        )

    away = [(apart, to_core) for apart in range(1, chips) for to_core in range(2)]

    make_hidden(0)
    pl.semaphore_wait(barrier, n_dp - 1 + n_sp - 1)
    send_own(0)

    dout_load.wait()

    def slot_step(step, carry):
        cols = pl.ds(pl.multiple_of(step * tn, tn), tn)
        picked = jnp.dot(choose_slot[...], dout[:, cols], preferred_element_type=f32)
        dcyc[sp, :, cols] = (slot_weight[...] * picked).astype(bf)
        return carry

    lax.fori_loop(0, n_col, slot_step, 0)

    relayed = n_sp == 4
    if relayed:
        near = [sp + 1 - 2 * lax.rem(sp, 2), lax.rem(sp + 2, 4)]
    else:
        near = [lax.rem(sp + off, n_sp) for off in range(1, n_sp)]
    ways = range(len(near))
    half_rows, half_dp = slot_rows // 2, (n_dp - 2) // 2

    def g_send(way):
        return remote(dcyc.at[sp], dcyc.at[sp], gsend.at[way], grecv.at[sp], sp=near[way])

    def b_send(way):
        return remote(dall.at[2:, sp], dall.at[2:, sp], bsend.at[way], brecv.at[sp], sp=near[way])

    def g_half(source, way):
        return dcyc.at[source, way * half_rows:(way + 1) * half_rows]

    def b_half(source, way):
        return dall.at[2 + way * half_dp:2 + (way + 1) * half_dp, source]

    def g_pass(way):
        held = g_half(near[way], way)
        return remote(held, held, fsend.at[way], frecv.at[way], sp=near[1 - way])

    def b_pass(way):
        held = b_half(near[way], way)
        return remote(held, held, fsend.at[2 + way], frecv.at[2 + way], sp=near[1 - way])

    for way in ways:
        g_send(way).start()
    for p in range(1, PIECES):
        make_hidden(p)
        send_own(p)
    for apart, to_core in away:
        a_send(apart, to_core).start()

    def r_send(step, off):
        other = lax.rem(sp + off, n_sp)
        cols = pl.ds(pl.multiple_of(step * tn, tn), tn)
        return remote(
            part.at[other, :, cols], rs_ref.at[sp, :, cols],
            rsend.at[step, off], rrecv.at[step, sp], sp=other,
        )

    def half_cols(step, way):
        half = tn // 2
        return pl.ds(pl.multiple_of(step * tn + way * half, half), half)

    def r_hop(step, way, kind):
        cols = half_cols(step, way)
        src = [part.at[near[way], :, cols], part.at[3 - sp, :, cols], rs_ref.at[3, :, cols]][kind]
        return remote(
            src, rs_ref.at[kind, :, cols], rsend.at[step, 2 * kind + way], rrecv.at[step, 2 * kind + way],
            sp=near[1 - way if kind == 2 else way],
        )

    def r_arrived(step, way, kind):
        arrived(rs_ref.at[kind, :, half_cols(step, way)], rrecv.at[step, 2 * kind + way])

    def fold_step(step, carry):
        for way in range(2):
            cols = half_cols(step, way)
            r_arrived(step, way, 1)
            rs_ref[3, :, cols] = (
                part[near[1 - way], :, cols].astype(f32) + rs_ref[1, :, cols].astype(f32)
            ).astype(bf)
            r_hop(step, way, 2).start()
        return carry

    def col_step(step, carry):
        slot = lax.rem(step, 2)

        @pl.when(step + 1 < n_col)
        def _():
            col_load(step + 1, 1 - slot).start()

        col_load(step, slot).wait()
        cols = pl.ds(pl.multiple_of(step * tn, tn), tn)
        product = jnp.dot(hall[dp], wcol[slot], preferred_element_type=f32)
        part[:, :, cols] = product.astype(bf).reshape(n_sp, slot_rows, tn)
        if relayed:
            for kind in (1, 0):
                for way in range(2):
                    r_hop(step, way, kind).start()
        else:
            for off in range(1, n_sp):
                r_send(step, off).start()
        return carry

    lax.fori_loop(0, n_col, col_step, 0)

    def relay(step, p):
        @pl.when(chip - step >= 0)
        def _():
            index = dp - 2 * step
            h_wait(index, p)

            @pl.when(chip + 1 < chips)
            def _():
                h_right(index, p, step).start()

            h_pair(index, p).start()

        @pl.when(chip + step < chips)
        def _():
            index = dp + 2 * step
            h_wait(index, p)

            @pl.when(chip >= 1)
            def _():
                h_left(index, p, step).start()

            h_pair(index, p).start()

    last = chips - 1
    for p in range(PIECES - 1):
        if last > 1:
            relay(1, p)
    for way in ways:
        arrived(dcyc.at[near[way]], grecv.at[near[way]])
        if relayed:
            g_pass(way).start()
    if last > 1:
        relay(1, PIECES - 1)

    if relayed:
        lax.fori_loop(0, n_col, fold_step, 0)

    for slot in range(2, n_dp):
        arrived(dall.at[slot, sp], arecv.at[slot])
    for way in ways:
        b_send(way).start()

    if relayed:
        for way in ways:
            arrived(g_half(3 - sp, way), frecv.at[way])

    own_copy = pltpu.make_async_copy(dcyc.at[:, :, block_cols(dp)], dall.at[core], local_sem.at[0])
    mate_copy = remote(
        dcyc.at[:, :, block_cols(partner)], dall.at[core], mate_send.at[0], arecv.at[core], dp=partner
    )
    own_copy.start()
    mate_copy.start()

    def row_step(step, carry):
        slot = lax.rem(step, 2)

        @pl.when(step + 1 < n_row)
        def _():
            row_load(step + 1, 1 - slot).start()

        row_load(step, slot).wait()
        cols = pl.ds(pl.multiple_of(step * th, th), th)
        d_hidden = lax.dot_general(
            dcyc[...].reshape(slots, width), wrow[slot], (((1,), (1,)), ((), ())), preferred_element_type=f32
        )
        gate_wide, up_wide = gate[:, cols].astype(f32), up[:, cols].astype(f32)
        sigma = jax.nn.sigmoid(gate_wide)
        ggrad_ref[:, cols] = (d_hidden * up_wide * sigma * (1.0 + gate_wide * (1.0 - sigma))).astype(bf)
        ugrad_ref[:, cols] = (d_hidden * (gate_wide * sigma)).astype(bf)
        return carry

    for p in range(PIECES):
        lax.fori_loop(p * n_row // PIECES, (p + 1) * n_row // PIECES, row_step, 0)
        if last > 2:
            relay(2, p)

    wide = 256 if block % 256 == 0 else 128
    half_slots, half_sp = slots // 2, n_sp // 2

    def down_pass(source, half, initial):
        rel = lax.rem(source - chip + chips, chips)
        span, here, owners = slots, slice(None), slice(None)
        if half is not None:
            span = half_slots
            here, owners = slice(half * half_slots, (half + 1) * half_slots), slice(half * half_sp, (half + 1) * half_sp)

        left = hall[pl.ds(2 * source, 2), here].reshape(2 * span, hid_width)
        for start in range(0, block, wide):
            cols = slice(start, start + wide)
            product = lax.dot_general(
                left, dall[pl.ds(2 * rel, 2), owners, :, cols].reshape(2 * span, wide),
                (((0,), (0,)), ((), ())), preferred_element_type=f32,
            )
            if initial:
                down_ref[:, cols] = product
            else:
                down_ref[:, cols] += product

    own_copy.wait()
    arrived(dall.at[1 - core], arecv.at[1 - core])
    for p in range(PIECES):
        h_wait(partner, p)
    down_pass(chip, None, True)

    wgrad[...] = jnp.zeros_like(wgrad)

    def mix_step(step, carry):
        cols = pl.ds(pl.multiple_of(step * tn, tn), tn)
        total = part[sp, :, cols].astype(f32)
        if relayed:
            for kind in (0, 2):
                for way in range(2):
                    r_arrived(step, way, kind)
                total = total + rs_ref[kind, :, cols].astype(f32)
        else:
            for off in range(1, n_sp):
                other = lax.rem(sp + off, n_sp)
                arrived(rs_ref.at[other, :, cols], rrecv.at[step, other])
                total = total + rs_ref[other, :, cols].astype(f32)
        high = total.astype(bf)
        low = (total - high.astype(f32)).astype(bf)
        choose = choose_tok[:, :slot_rows]
        token_out = jnp.dot(choose, high, preferred_element_type=f32) + jnp.dot(
            choose, low, preferred_element_type=f32
        )
        mixed_ref[:, cols] = (token_weight[:, 0:1] * token_out).astype(bf)
        wgrad[...] += jnp.sum(dout[:, cols].astype(f32) * token_out, axis=1, keepdims=True)
        if relayed:
            for kind in range(3):
                for way in range(2):
                    r_hop(step, way, kind).wait_send()
        else:
            for off in range(1, n_sp):
                r_send(step, off).wait_send()
        return carry

    lax.fori_loop(0, n_col, mix_step, 0)

    slope = jnp.transpose(jnp.broadcast_to(wgrad[...], (tokens, tokens)))[0:1, :] * weight * (1.0 - weight)
    first_col = jnp.where(first > 0.0, slope, -slope)
    lgrad_ref[0:1, :] = first_col
    lgrad_ref[1:2, :] = -first_col

    for way in ways:
        arrived(dall.at[2:, near[way]], brecv.at[near[way]])
        if relayed:
            b_pass(way).start()

    for step in range(3, last):
        for p in range(PIECES):
            relay(step, p)

    if relayed:
        for way in ways:
            arrived(b_half(3 - sp, way), frecv.at[2 + way])

    def down_step(index, carry):
        source = chip + (lax.div(index, 2) + 1) * (2 * lax.rem(index, 2) - 1)

        @pl.when((source >= 0) & (source < chips))
        def _():
            for p in range(PIECES):
                h_wait(2 * source + 1 - core, p)
            down_pass(source, None, False)

        return carry

    if last > 1:
        lax.fori_loop(0, 2 * (last - 1), down_step, 0)

    if last > 0:
        @pl.when((chip == 0) | (chip == last))
        def _():
            source = last - chip
            for half in range(2):
                mine = range(half * PIECES // 2, (half + 1) * PIECES // 2)
                for p in mine:
                    h_wait(2 * source + core, p)
                    h_pair(2 * source + core, p).start()
                for p in mine:
                    h_wait(2 * source + 1 - core, p)
                down_pass(source, half, False)

    mate_copy.wait_send()
    for way in ways:
        g_send(way).wait_send()
        b_send(way).wait_send()
        if relayed:
            g_pass(way).wait_send()
            b_pass(way).wait_send()
    for apart, to_core in away:
        a_send(apart, to_core).wait_send()
    for step in range(chips):
        for p in range(PIECES):
            @pl.when((chip - step >= 0) & (chip + 1 < chips))
            def _():
                h_right(dp, p, step).wait_send()

            @pl.when((chip + step < chips) & (chip >= 1))
            def _():
                h_left(dp, p, step).wait_send()

            h_send(dp, p, partner, pair_send.at[PIECES * step + p]).wait_send()


def fused(n_dp, n_sp, ids, logits, gate_pre, up_pre, w_down, d_out):
    slots, hid_width = gate_pre.shape
    tokens, width = d_out.shape
    slot_rows = slots // n_sp
    block = width // n_dp
    tn, th = width // 8, min(256, hid_width)
    n_col = width // tn
    chips = n_dp // 2
    f32, bf = jnp.float32, jnp.bfloat16
    dma = pltpu.SemaphoreType.DMA
    hbm = pl.BlockSpec(memory_space=pl.ANY)
    vmem = pl.BlockSpec(memory_space=pltpu.VMEM)
    buffers = [
        ((slots, hid_width), bf), ((slots, hid_width), bf), ((tokens, width), bf),
        ((n_dp, slots, hid_width), bf), ((n_dp, n_sp, slot_rows, block), bf),
        ((n_sp, slot_rows, width), bf), ((n_sp, slot_rows, width), bf), ((n_sp, slot_rows, width), bf),
        ((2, hid_width, tn), bf), ((2, th, width), bf),
        ((slot_rows, tokens), bf), ((slot_rows, 1), f32), ((tokens, tokens), bf), ((tokens, tokens), f32),
        ((tokens, 1), f32),
    ]
    results = [
        ((tokens, width), bf), ((2, tokens), f32), ((slots, hid_width), bf), ((slots, hid_width), bf),
        ((hid_width, block), f32),
    ]
    kept = sum(math.prod(shape) * jnp.dtype(dtype).itemsize for shape, dtype in results)
    return pl.pallas_call(
        functools.partial(fused_kernel, n_dp, n_sp),
        out_shape=tuple(pltpu.VMEM(shape, dtype) for shape, dtype in results),
        in_specs=[vmem, vmem, hbm, hbm, hbm, hbm],
        out_specs=(vmem,) * 5,
        scratch_shapes=[pltpu.VMEM(shape, dtype) for shape, dtype in buffers] + [
            dma((2 * PIECES + 1,)),
            dma((4,)),
            dma((1,)),
            dma((PIECES * chips,)),
            dma((PIECES * chips,)),
            dma((PIECES * chips,)),
            dma((PIECES * n_dp,)),
            dma((n_dp,)),
            dma((n_dp,)),
            dma((n_sp,)),
            dma((n_sp,)),
            dma((n_sp,)),
            dma((n_sp,)),
            dma((n_col, max(n_sp, 6))),
            dma((n_col, max(n_sp, 6))),
            dma((4,)),
            dma((4,)),
            dma((1,)),
        ],
        compiler_params=pltpu.CompilerParams(
            collective_id=0, has_side_effects=True, vmem_limit_bytes=62 * 1024 * 1024 - kept
        ),
    )(ids, logits, gate_pre, up_pre, w_down, d_out)


def emit_kernel(*refs):
    count = len(refs) // 2
    sems = refs[-1]
    copies = [pltpu.make_async_copy(refs[i], refs[count + i], sems.at[i]) for i in range(count)]
    for copy in copies:
        copy.start()
    for copy in copies:
        copy.wait()


def emit(*arrays):
    return pl.pallas_call(
        emit_kernel,
        out_shape=tuple(jax.ShapeDtypeStruct(array.shape, array.dtype) for array in arrays),
        in_specs=[pl.BlockSpec(memory_space=pltpu.VMEM)] * len(arrays),
        out_specs=(pl.BlockSpec(memory_space=pl.ANY),) * len(arrays),
        scratch_shapes=[pltpu.SemaphoreType.DMA((len(arrays),))],
        compiler_params=pltpu.CompilerParams(vmem_limit_bytes=1024 * 1024),
    )(*[pltpu.with_memory_space_constraint(array, pltpu.VMEM) for array in arrays])


def local(n_dp, n_sp, gate_pre, up_pre, w_down, route_logits, expert_ids, d_out):
    mixed, slopes, gate_grads, up_grads, down_grads = emit(*fused(
        n_dp, n_sp, expert_ids.T, route_logits.T, gate_pre, up_pre, w_down, d_out
    ))
    return (mixed, slopes.T, gate_grads, up_grads, down_grads)


def solution(mesh):
    both = P(("dp", "sp"), None)
    return jax.shard_map(
        functools.partial(local, mesh.shape["dp"], mesh.shape["sp"]),
        mesh=mesh,
        in_specs=(P("dp", "sp"), P("dp", "sp"), P("sp", None), both, both, both),
        out_specs=(both, both, P("dp", "sp"), P("dp", "sp"), P("sp", "dp")),
        check_vma=False,
    )
```

```python
import functools
import math

import jax
import jax.numpy as jnp
from jax import lax
from jax.experimental import pallas as pl
from jax.experimental.pallas import tpu as pltpu
from jax.sharding import PartitionSpec as P

MESH = pl.DeviceIdType.MESH
CUTS = (0, 1, 3, 5, 7, 8)
PIECES = len(CUTS) - 1
LATE = 2
CHUNKS = 4


def fused_kernel(
    n_dp, n_sp, ids_hbm, logit_hbm, gate_hbm, up_hbm, w_ref, dout_hbm,
    mixed_ref, lgrad_ref, ggrad_ref, ugrad_ref, down_ref, late_hid, late_cot,
    ids_ref, logit_ref, gate, up, dout, hall, dall, dcyc, part, rs_ref, wcol, wrow,
    choose_slot, slot_weight, choose_tok, token_weight, wgrad,
    load_sem, wsem, local_sem, right_send, left_send, pair_send, hrecv, asend, arecv,
    gsend, grecv, bsend, brecv, rsend, rrecv, fsend, frecv, mate_send,
):
    f32, bf = jnp.float32, jnp.bfloat16
    dp, sp = lax.axis_index("dp"), lax.axis_index("sp")
    chips = n_dp // 2
    chip, core = lax.div(dp, 2), lax.rem(dp, 2)
    partner = chip * 2 + 1 - core
    slots, hid_width = gate.shape
    tokens, width = dout.shape
    slot_rows = dcyc.shape[1]
    block = width // n_dp
    bounds = [cut * slots // CUTS[-1] for cut in CUTS]
    early = bounds[PIECES - LATE]
    late = slots - early
    tn = wcol.shape[2]
    th = wrow.shape[1]
    n_col, n_row = width // tn, hid_width // th

    def piece_rows(p):
        return slice(bounds[p], bounds[p + 1])

    def gate_load(p):
        return pltpu.make_async_copy(gate_hbm.at[piece_rows(p)], gate.at[piece_rows(p)], load_sem.at[2 * p])

    def up_load(p):
        return pltpu.make_async_copy(up_hbm.at[piece_rows(p)], up.at[piece_rows(p)], load_sem.at[2 * p + 1])

    ids_load = pltpu.make_async_copy(ids_hbm, ids_ref, load_sem.at[2 * PIECES + 1])
    logit_load = pltpu.make_async_copy(logit_hbm, logit_ref, load_sem.at[2 * PIECES + 2])
    dout_load = pltpu.make_async_copy(dout_hbm, dout, load_sem.at[2 * PIECES])

    def col_load(step, slot):
        return pltpu.make_async_copy(
            w_ref.at[:, pl.ds(pl.multiple_of(step * tn, tn), tn)], wcol.at[slot], wsem.at[slot]
        )

    def row_load(step, slot):
        return pltpu.make_async_copy(
            w_ref.at[pl.ds(pl.multiple_of(step * th, th), th), :], wrow.at[slot], wsem.at[2 + slot]
        )

    gate_load(0).start()
    up_load(0).start()
    barrier = pltpu.get_barrier_semaphore()
    for off in range(1, n_dp):
        pl.semaphore_signal(barrier, inc=1, device_id={"dp": lax.rem(dp + off, n_dp)}, device_id_type=MESH)
    for off in range(1, n_sp):
        pl.semaphore_signal(barrier, inc=1, device_id={"sp": lax.rem(sp + off, n_sp)}, device_id_type=MESH)
    ids_load.start()
    logit_load.start()
    dout_load.start()
    for p in range(1, PIECES):
        gate_load(p).start()
        up_load(p).start()
    col_load(0, 0).start()
    row_load(0, 0).start()

    def remote(src, dst, send, recv, **where):
        return pltpu.make_async_remote_copy(
            src_ref=src, dst_ref=dst, send_sem=send, recv_sem=recv, device_id=where, device_id_type=MESH
        )

    def arrived(ref, sem):
        pltpu.make_async_copy(ref, ref, sem).wait()

    def block_cols(index):
        return pl.ds(pl.multiple_of(index * block, block), block)

    def make_hidden(p):
        gate_load(p).wait()
        up_load(p).wait()

        def step(i, carry):
            here = pl.ds(pl.multiple_of(bounds[p] + i * 16, 16), 16)
            gate_wide = gate[here, :].astype(f32)
            silu = gate_wide * jax.nn.sigmoid(gate_wide)
            hall[dp, here, :] = (silu * up[here, :].astype(f32)).astype(bf)
            return carry

        lax.fori_loop(0, (bounds[p + 1] - bounds[p]) // 16, step, 0)

    def piece(index, p):
        return hall.at[index, piece_rows(p)]

    def h_send(index, p, to, send):
        return remote(piece(index, p), piece(index, p), send, hrecv.at[PIECES * index + p], dp=to)

    def h_wait(index, p):
        arrived(piece(index, p), hrecv.at[PIECES * index + p])

    def h_right(index, p, step):
        return h_send(index, p, dp + 2, right_send.at[PIECES * step + p])

    def h_left(index, p, step):
        return h_send(index, p, dp - 2, left_send.at[PIECES * step + p])

    def h_pair(index, p):
        return h_send(index, p, partner, pair_send.at[PIECES * lax.div(index, 2) + p])

    def send_own(p):
        @pl.when(chip + 1 < chips)
        def _():
            h_right(dp, p, 0).start()

        @pl.when(chip >= 1)
        def _():
            h_left(dp, p, 0).start()

        h_pair(dp, p).start()

    def a_send(apart, to_core):
        other = 2 * lax.rem(chip + apart, chips) + to_core
        return remote(
            dcyc.at[sp, :, block_cols(other)], dall.at[2 * (chips - apart) + core, sp],
            asend.at[2 * apart + to_core], arecv.at[2 * (chips - apart) + core], dp=other,
        )

    away = [(apart, to_core) for apart in range(1, chips) for to_core in range(2)]

    make_hidden(0)
    pl.semaphore_wait(barrier, n_dp - 1 + n_sp - 1)
    send_own(0)

    ids_load.wait()
    logit_load.wait()
    zero = (ids_ref[...] == 0).astype(f32)
    first, second = zero[0:1, :], zero[1:2, :]
    routed = jnp.maximum(first, second)
    logits = logit_ref[...]
    own_logit = jnp.where(first > 0.0, logits[0:1, :], logits[1:2, :])
    other_logit = jnp.where(first > 0.0, logits[1:2, :], logits[0:1, :])
    weight = routed * jax.nn.sigmoid(own_logit - other_logit)
    along = lax.broadcasted_iota(jnp.int32, (tokens, tokens), 0)
    across = lax.broadcasted_iota(jnp.int32, (tokens, tokens), 1)
    before = jnp.where(along <= across, 1.0, 0.0).astype(bf)
    rank = jnp.dot(jnp.broadcast_to(routed, (16, tokens)).astype(bf), before, preferred_element_type=f32)[0:1, :] - 1.0
    chooser = jnp.where(along.astype(f32) == rank, 1.0, 0.0) * routed
    choose_slot[...] = chooser[:slot_rows, :].astype(bf)
    slot_weight[...] = jnp.sum(chooser[:slot_rows, :] * weight, axis=1, keepdims=True)
    choose_tok[...] = jnp.transpose(chooser).astype(bf)
    token_weight[...] = jnp.transpose(jnp.broadcast_to(weight, (tokens, tokens)))

    dout_load.wait()

    def slot_step(step, carry):
        cols = pl.ds(pl.multiple_of(step * tn, tn), tn)
        picked = jnp.dot(choose_slot[...], dout[:, cols], preferred_element_type=f32)
        dcyc[sp, :, cols] = (slot_weight[...] * picked).astype(bf)
        return carry

    lax.fori_loop(0, n_col, slot_step, 0)

    relayed = n_sp == 4
    if relayed:
        near = [sp + 1 - 2 * lax.rem(sp, 2), lax.rem(sp + 2, 4)]
    else:
        near = [lax.rem(sp + off, n_sp) for off in range(1, n_sp)]
    ways = range(len(near))
    half_rows, half_dp = slot_rows // 2, (n_dp - 2) // 2

    def g_send(way):
        return remote(dcyc.at[sp], dcyc.at[sp], gsend.at[way], grecv.at[sp], sp=near[way])

    def b_send(way):
        return remote(dall.at[2:, sp], dall.at[2:, sp], bsend.at[way], brecv.at[sp], sp=near[way])

    def g_half(source, way):
        return dcyc.at[source, way * half_rows:(way + 1) * half_rows]

    def b_half(source, way):
        return dall.at[2 + way * half_dp:2 + (way + 1) * half_dp, source]

    def g_pass(way):
        held = g_half(near[way], way)
        return remote(held, held, fsend.at[way], frecv.at[way], sp=near[1 - way])

    def b_pass(way):
        held = b_half(near[way], way)
        return remote(held, held, fsend.at[2 + way], frecv.at[2 + way], sp=near[1 - way])

    for way in ways:
        g_send(way).start()
    for apart, to_core in away:
        a_send(apart, to_core).start()
    for p in range(1, PIECES):
        make_hidden(p)
        send_own(p)
    late_hid[...] = jnp.zeros_like(late_hid)
    late_cot[...] = jnp.zeros_like(late_cot)

    def r_send(step, off):
        other = lax.rem(sp + off, n_sp)
        cols = pl.ds(pl.multiple_of(step * tn, tn), tn)
        return remote(
            part.at[other, :, cols], rs_ref.at[sp, :, cols],
            rsend.at[step, off], rrecv.at[step, sp], sp=other,
        )

    def half_cols(step, way):
        half = tn // 2
        return pl.ds(pl.multiple_of(step * tn + way * half, half), half)

    def r_hop(step, way, kind):
        cols = half_cols(step, way)
        src = [part.at[near[way], :, cols], part.at[3 - sp, :, cols], rs_ref.at[3, :, cols]][kind]
        return remote(
            src, rs_ref.at[kind, :, cols], rsend.at[step, 2 * kind + way], rrecv.at[step, 2 * kind + way],
            sp=near[1 - way if kind == 2 else way],
        )

    def r_arrived(step, way, kind):
        arrived(rs_ref.at[kind, :, half_cols(step, way)], rrecv.at[step, 2 * kind + way])

    def fold_step(step, carry):
        for way in range(2):
            cols = half_cols(step, way)
            r_arrived(step, way, 1)
            rs_ref[3, :, cols] = (
                part[near[1 - way], :, cols].astype(f32) + rs_ref[1, :, cols].astype(f32)
            ).astype(bf)
            r_hop(step, way, 2).start()
        return carry

    def col_step(step, carry):
        slot = lax.rem(step, 2)

        @pl.when(step + 1 < n_col)
        def _():
            col_load(step + 1, 1 - slot).start()

        col_load(step, slot).wait()
        cols = pl.ds(pl.multiple_of(step * tn, tn), tn)
        product = jnp.dot(hall[dp], wcol[slot], preferred_element_type=f32)
        part[:, :, cols] = product.astype(bf).reshape(n_sp, slot_rows, tn)
        return carry

    lax.fori_loop(0, n_col, col_step, 0)

    def part_sends(kind):
        def step_sends(step, carry):
            if relayed:
                for way in range(2):
                    r_hop(step, way, kind).start()
            else:
                for off in range(1, n_sp):
                    r_send(step, off).start()
            return carry

        lax.fori_loop(0, n_col, step_sends, 0)

    def relay(step, p):
        @pl.when(chip - step >= 0)
        def _():
            index = dp - 2 * step
            h_wait(index, p)

            @pl.when(chip + 1 < chips)
            def _():
                h_right(index, p, step).start()

            h_pair(index, p).start()

        @pl.when(chip + step < chips)
        def _():
            index = dp + 2 * step
            h_wait(index, p)

            @pl.when(chip >= 1)
            def _():
                h_left(index, p, step).start()

            h_pair(index, p).start()

    last = chips - 1
    for slot in range(2, n_dp):
        arrived(dall.at[slot, sp], arecv.at[slot])
    for way in ways:
        b_send(way).start()
    for way in ways:
        arrived(dcyc.at[near[way]], grecv.at[near[way]])
        if relayed:
            g_pass(way).start()
    part_sends(1)
    for p in range(PIECES - LATE):
        if last > 1:
            relay(1, p)
    for way in ways:
        arrived(dall.at[2:, near[way]], brecv.at[near[way]])
        if relayed:
            b_pass(way).start()
    if relayed:
        part_sends(0)
    for p in range(PIECES - LATE, PIECES):
        if last > 1:
            relay(1, p)

    if relayed:
        for way in ways:
            arrived(g_half(3 - sp, way), frecv.at[way])

    own_copy = pltpu.make_async_copy(dcyc.at[:, :, block_cols(dp)], dall.at[core], local_sem.at[0])
    mate_copy = remote(
        dcyc.at[:, :, block_cols(partner)], dall.at[core], mate_send.at[0], arecv.at[core], dp=partner
    )
    own_copy.start()
    mate_copy.start()

    def row_step(step, carry):
        slot = lax.rem(step, 2)

        @pl.when(step + 1 < n_row)
        def _():
            row_load(step + 1, 1 - slot).start()

        row_load(step, slot).wait()
        cols = pl.ds(pl.multiple_of(step * th, th), th)
        d_hidden = lax.dot_general(
            dcyc[...].reshape(slots, width), wrow[slot], (((1,), (1,)), ((), ())), preferred_element_type=f32
        )
        gate_wide, up_wide = gate[:, cols].astype(f32), up[:, cols].astype(f32)
        sigma = jax.nn.sigmoid(gate_wide)
        ggrad_ref[:, cols] = (d_hidden * up_wide * sigma * (1.0 + gate_wide * (1.0 - sigma))).astype(bf)
        ugrad_ref[:, cols] = (d_hidden * (gate_wide * sigma)).astype(bf)
        return carry

    for p in range(PIECES):
        lax.fori_loop(p * n_row // PIECES, (p + 1) * n_row // PIECES, row_step, 0)
        if last > 2:
            relay(2, p)
        if relayed and p == 1:
            lax.fori_loop(0, n_col, fold_step, 0)

    wide = 256 if block % 256 == 0 else 128

    def cotangents(source, cols):
        rel = lax.rem(source - chip + chips, chips)
        return dall[pl.ds(2 * rel, 2), :, :, cols].reshape(2, slots, -1)

    def down_pass(source, span, initial):
        left = hall[pl.ds(2 * source, 2), :span].reshape(2 * span, hid_width)
        for start in range(0, block, wide):
            cols = slice(start, start + wide)
            product = lax.dot_general(
                left, cotangents(source, cols)[:, :span].reshape(2 * span, wide),
                (((0,), (0,)), ((), ())), preferred_element_type=f32,
            )
            if initial:
                down_ref[:, cols] = product
            else:
                down_ref[:, cols] += product

    own_copy.wait()
    arrived(dall.at[1 - core], arecv.at[1 - core])
    for p in range(PIECES):
        h_wait(partner, p)
    down_pass(chip, slots, True)

    wgrad[...] = jnp.zeros_like(wgrad)

    def mix_step(step, carry):
        cols = pl.ds(pl.multiple_of(step * tn, tn), tn)
        total = part[sp, :, cols].astype(f32)
        if relayed:
            for kind in (0, 2):
                for way in range(2):
                    r_arrived(step, way, kind)
                total = total + rs_ref[kind, :, cols].astype(f32)
        else:
            for off in range(1, n_sp):
                other = lax.rem(sp + off, n_sp)
                arrived(rs_ref.at[other, :, cols], rrecv.at[step, other])
                total = total + rs_ref[other, :, cols].astype(f32)
        high = total.astype(bf)
        low = (total - high.astype(f32)).astype(bf)
        choose = choose_tok[:, :slot_rows]
        token_out = jnp.dot(choose, high, preferred_element_type=f32) + jnp.dot(
            choose, low, preferred_element_type=f32
        )
        mixed_ref[:, cols] = (token_weight[:, 0:1] * token_out).astype(bf)
        wgrad[...] += jnp.sum(dout[:, cols].astype(f32) * token_out, axis=1, keepdims=True)
        if relayed:
            for kind in range(3):
                for way in range(2):
                    r_hop(step, way, kind).wait_send()
        else:
            for off in range(1, n_sp):
                r_send(step, off).wait_send()
        return carry

    for step in range(3, last):
        for p in range(PIECES):
            relay(step, p)

    if relayed:
        for way in ways:
            arrived(b_half(3 - sp, way), frecv.at[2 + way])

    def down_step(index, carry):
        source = chip + (lax.div(index, 2) + 1) * (2 * lax.rem(index, 2) - 1)

        @pl.when((source >= 0) & (source < chips))
        def _():
            for p in range(PIECES):
                h_wait(2 * source + 1 - core, p)
            down_pass(source, slots, False)

        return carry

    if last > 1:
        lax.fori_loop(0, 2 * (last - 1), down_step, 0)

    ends = (chip == 0) | (chip == last)
    far = last - chip

    def forward(p):
        @pl.when(ends)
        def _():
            h_wait(2 * far + core, p)
            h_pair(2 * far + core, p).start()

    for p in range(2):
        forward(p)

    lax.fori_loop(0, n_col, mix_step, 0)

    slope = jnp.transpose(jnp.broadcast_to(wgrad[...], (tokens, tokens)))[0:1, :] * weight * (1.0 - weight)
    first_col = jnp.where(first > 0.0, slope, -slope)
    lgrad_ref[0:1, :] = first_col
    lgrad_ref[1:2, :] = -first_col

    mate_copy.wait_send()
    for way in ways:
        g_send(way).wait_send()
        b_send(way).wait_send()
        if relayed:
            g_pass(way).wait_send()
            b_pass(way).wait_send()
    for apart, to_core in away:
        a_send(apart, to_core).wait_send()

    def sent(step, p):
        @pl.when((chip - step >= 0) & (chip + 1 < chips))
        def _():
            h_right(dp, p, step).wait_send()

        @pl.when((chip + step < chips) & (chip >= 1))
        def _():
            h_left(dp, p, step).wait_send()

    for p in range(PIECES):
        for step in range(last):
            sent(step, p)

    for p in range(2, PIECES - LATE):
        forward(p)

    @pl.when(ends)
    def _():
        for p in range(PIECES - LATE):
            h_wait(2 * far + 1 - core, p)
        down_pass(far, early, False)
        late_cot[...] = cotangents(far, slice(None))[:, early:].reshape(2 * late, block)

    for p in range(PIECES - LATE, PIECES):
        forward(p)

    @pl.when(ends)
    def _():
        for p in range(PIECES - LATE, PIECES):
            h_wait(2 * far + 1 - core, p)
        late_hid[...] = hall[pl.ds(2 * far, 2), early:].reshape(2 * late, hid_width)

    for step in range(chips):
        for p in range(PIECES):
            h_send(dp, p, partner, pair_send.at[PIECES * step + p]).wait_send()


def fused(n_dp, n_sp, ids, logits, gate_pre, up_pre, w_down, d_out):
    slots, hid_width = gate_pre.shape
    tokens, width = d_out.shape
    slot_rows = slots // n_sp
    block = width // n_dp
    tn, th = width // 8, min(256, hid_width // 8)
    n_col = width // tn
    chips = n_dp // 2
    late = slots - CUTS[-1 - LATE] * slots // CUTS[-1]
    f32, bf = jnp.float32, jnp.bfloat16
    dma = pltpu.SemaphoreType.DMA
    hbm = pl.BlockSpec(memory_space=pl.ANY)
    vmem = pl.BlockSpec(memory_space=pltpu.VMEM)
    buffers = [
        (ids.shape, ids.dtype), (logits.shape, logits.dtype),
        ((slots, hid_width), bf), ((slots, hid_width), bf), ((tokens, width), bf),
        ((n_dp, slots, hid_width), bf), ((n_dp, n_sp, slot_rows, block), bf),
        ((n_sp, slot_rows, width), bf), ((n_sp, slot_rows, width), bf), ((n_sp, slot_rows, width), bf),
        ((2, hid_width, tn), bf), ((2, th, width), bf),
        ((slot_rows, tokens), bf), ((slot_rows, 1), f32), ((tokens, tokens), bf), ((tokens, tokens), f32),
        ((tokens, 1), f32),
    ]
    results = [
        ((tokens, width), bf), ((2, tokens), f32), ((slots, hid_width), bf), ((slots, hid_width), bf),
        ((hid_width, block), f32), ((2 * late, hid_width), bf), ((2 * late, block), bf),
    ]
    kept = sum(math.prod(shape) * jnp.dtype(dtype).itemsize for shape, dtype in results)
    return pl.pallas_call(
        functools.partial(fused_kernel, n_dp, n_sp),
        out_shape=tuple(pltpu.VMEM(shape, dtype) for shape, dtype in results),
        in_specs=[hbm] * 6,
        out_specs=(vmem,) * 7,
        scratch_shapes=[pltpu.VMEM(shape, dtype) for shape, dtype in buffers] + [
            dma((2 * PIECES + 3,)),
            dma((4,)),
            dma((1,)),
            dma((PIECES * chips,)),
            dma((PIECES * chips,)),
            dma((PIECES * chips,)),
            dma((PIECES * n_dp,)),
            dma((n_dp,)),
            dma((n_dp,)),
            dma((n_sp,)),
            dma((n_sp,)),
            dma((n_sp,)),
            dma((n_sp,)),
            dma((n_col, max(n_sp, 6))),
            dma((n_col, max(n_sp, 6))),
            dma((4,)),
            dma((4,)),
            dma((1,)),
        ],
        compiler_params=pltpu.CompilerParams(
            collective_id=0, has_side_effects=True, vmem_limit_bytes=62 * 1024 * 1024 - kept
        ),
    )(ids, logits, gate_pre, up_pre, w_down, d_out)


def finish_kernel(
    mixed_ref, slopes_ref, ggrad_ref, ugrad_ref, down_ref, late_hid, late_cot,
    mixed_out, slopes_out, ggrad_out, ugrad_out, down_out, total, sems,
):
    done = [(mixed_ref, mixed_out), (slopes_ref, slopes_out), (ggrad_ref, ggrad_out), (ugrad_ref, ugrad_out)]
    copies = [pltpu.make_async_copy(src, dst, sems.at[i]) for i, (src, dst) in enumerate(done)]
    for copy in copies:
        copy.start()
    span = total.shape[0] // CHUNKS
    for chunk in range(CHUNKS):
        here = slice(chunk * span, (chunk + 1) * span)
        total[here] = down_ref[here] + lax.dot_general(
            late_hid[:, here], late_cot[...], (((0,), (0,)), ((), ())), preferred_element_type=jnp.float32
        )
        copies.append(pltpu.make_async_copy(total.at[here], down_out.at[here], sems.at[len(done) + chunk]))
        copies[-1].start()
    for copy in copies:
        copy.wait()


def finish(*arrays):
    down = arrays[4]
    return pl.pallas_call(
        finish_kernel,
        out_shape=tuple(jax.ShapeDtypeStruct(array.shape, array.dtype) for array in arrays[:5]),
        in_specs=[pl.BlockSpec(memory_space=pltpu.VMEM)] * len(arrays),
        out_specs=(pl.BlockSpec(memory_space=pl.ANY),) * 5,
        scratch_shapes=[pltpu.VMEM(down.shape, down.dtype), pltpu.SemaphoreType.DMA((4 + CHUNKS,))],
        compiler_params=pltpu.CompilerParams(vmem_limit_bytes=16 * 1024 * 1024),
    )(*[pltpu.with_memory_space_constraint(array, pltpu.VMEM) for array in arrays])


def local(n_dp, n_sp, gate_pre, up_pre, w_down, route_logits, expert_ids, d_out):
    mixed, slopes, gate_grads, up_grads, down_grads = finish(*fused(
        n_dp, n_sp, expert_ids.T, route_logits.T, gate_pre, up_pre, w_down, d_out
    ))
    return (mixed, slopes.T, gate_grads, up_grads, down_grads)


def solution(mesh):
    both = P(("dp", "sp"), None)
    return jax.shard_map(
        functools.partial(local, mesh.shape["dp"], mesh.shape["sp"]),
        mesh=mesh,
        in_specs=(P("dp", "sp"), P("dp", "sp"), P("sp", None), both, both, both),
        out_specs=(both, both, P("dp", "sp"), P("dp", "sp"), P("sp", "dp")),
        check_vma=False,
    )
```

```python
import functools
import math

import jax
import jax.numpy as jnp
from jax import lax
from jax.experimental import pallas as pl
from jax.experimental.pallas import tpu as pltpu
from jax.sharding import PartitionSpec as P

MESH = pl.DeviceIdType.MESH
CUTS = (0, 1, 3, 5, 7, 8)
PIECES = len(CUTS) - 1
LATE = 2
CHUNKS = 4


def fused_kernel(
    n_dp, n_sp, ids_hbm, logit_hbm, gate_hbm, up_hbm, w_ref, dout_hbm,
    mixed_ref, lgrad_ref, ggrad_ref, ugrad_ref, down_ref, late_hid, late_cot,
    ids_ref, logit_ref, gate, up, dout, hall, dall, dcyc, part, rs_ref, wcol, wrow,
    choose_slot, slot_weight, choose_tok, token_weight, wgrad, shared,
    load_sem, wsem, local_sem, right_send, left_send, pair_send, hrecv, asend, arecv,
    gsend, grecv, bsend, brecv, rsend, rrecv, fsend, frecv, mate_send, mate_recv,
):
    f32, bf = jnp.float32, jnp.bfloat16
    dp, sp = lax.axis_index("dp"), lax.axis_index("sp")
    chips = n_dp // 2
    chip, core = lax.div(dp, 2), lax.rem(dp, 2)
    partner = chip * 2 + 1 - core
    slots, hid_width = gate.shape
    tokens, width = dout.shape
    slot_rows = dcyc.shape[1]
    block = width // n_dp
    bounds = [cut * slots // CUTS[-1] for cut in CUTS]
    early = bounds[PIECES - LATE]
    late = slots - early
    tn = wcol.shape[2]
    th = wrow.shape[1]
    n_col, n_row = width // tn, hid_width // th

    def piece_rows(p):
        return slice(bounds[p], bounds[p + 1])

    def gate_load(p):
        return pltpu.make_async_copy(gate_hbm.at[piece_rows(p)], gate.at[piece_rows(p)], load_sem.at[2 * p])

    def up_load(p):
        return pltpu.make_async_copy(up_hbm.at[piece_rows(p)], up.at[piece_rows(p)], load_sem.at[2 * p + 1])

    ids_load = pltpu.make_async_copy(ids_hbm, ids_ref, load_sem.at[2 * PIECES + 1])
    logit_load = pltpu.make_async_copy(logit_hbm, logit_ref, load_sem.at[2 * PIECES + 2])
    dout_load = pltpu.make_async_copy(dout_hbm, dout, load_sem.at[2 * PIECES])

    def col_load(step, slot):
        return pltpu.make_async_copy(
            w_ref.at[:, pl.ds(pl.multiple_of(step * tn, tn), tn)], wcol.at[slot], wsem.at[slot]
        )

    def row_load(step, slot):
        return pltpu.make_async_copy(
            w_ref.at[pl.ds(pl.multiple_of(step * th, th), th), :], wrow.at[slot], wsem.at[2 + slot]
        )

    gate_load(0).start()
    up_load(0).start()
    barrier = pltpu.get_barrier_semaphore()
    for apart in range(1, chips):
        pl.semaphore_signal(
            barrier, inc=1, device_id={"dp": 2 * lax.rem(chip + apart, chips) + core}, device_id_type=MESH
        )
    pl.semaphore_signal(barrier, inc=1, device_id={"dp": partner}, device_id_type=MESH)
    for off in range(1, n_sp):
        pl.semaphore_signal(barrier, inc=1, device_id={"sp": lax.rem(sp + off, n_sp)}, device_id_type=MESH)
    ids_load.start()
    logit_load.start()
    dout_load.start()
    for p in range(1, PIECES):
        gate_load(p).start()
        up_load(p).start()
    col_load(0, 0).start()
    row_load(0, 0).start()

    def remote(src, dst, send, recv, **where):
        return pltpu.make_async_remote_copy(
            src_ref=src, dst_ref=dst, send_sem=send, recv_sem=recv, device_id=where, device_id_type=MESH
        )

    def arrived(ref, sem):
        pltpu.make_async_copy(ref, ref, sem).wait()

    def block_cols(index):
        return pl.ds(pl.multiple_of(index * block, block), block)

    def make_hidden(p):
        gate_load(p).wait()
        up_load(p).wait()

        def step(i, carry):
            here = pl.ds(pl.multiple_of(bounds[p] + i * 16, 16), 16)
            gate_wide = gate[here, :].astype(f32)
            silu = gate_wide * jax.nn.sigmoid(gate_wide)
            hall[dp, here, :] = (silu * up[here, :].astype(f32)).astype(bf)
            return carry

        lax.fori_loop(0, (bounds[p + 1] - bounds[p]) // 16, step, 0)

    def piece(index, p):
        return hall.at[index, piece_rows(p)]

    def h_send(index, p, to, send):
        return remote(piece(index, p), piece(index, p), send, hrecv.at[PIECES * index + p], dp=to)

    def h_wait(index, p):
        arrived(piece(index, p), hrecv.at[PIECES * index + p])

    def h_right(index, p, step):
        return h_send(index, p, dp + 2, right_send.at[PIECES * step + p])

    def h_left(index, p, step):
        return h_send(index, p, dp - 2, left_send.at[PIECES * step + p])

    def h_pair(index, p):
        return h_send(index, p, partner, pair_send.at[PIECES * lax.div(index, 2) + p])

    def send_own(p):
        @pl.when(chip + 1 < chips)
        def _():
            h_right(dp, p, 0).start()

        @pl.when(chip >= 1)
        def _():
            h_left(dp, p, 0).start()

        h_pair(dp, p).start()

    def a_send(apart):
        other = lax.rem(chip + apart, chips)
        return remote(
            dcyc.at[sp, :, pl.ds(pl.multiple_of(other * 2 * block, 2 * block), 2 * block)], shared.at[chips - apart],
            asend.at[apart], arecv.at[chips - apart], dp=2 * other + core,
        )

    def a_own(rel):
        return pltpu.make_async_copy(
            shared.at[rel, :, block_cols(core)], dall.at[2 * rel + core, sp], local_sem.at[rel]
        )

    def a_mate(rel):
        return remote(
            shared.at[rel, :, block_cols(1 - core)], dall.at[2 * rel + core, sp],
            mate_send.at[rel], mate_recv.at[rel], dp=partner,
        )

    make_hidden(0)
    pl.semaphore_wait(barrier, chips + n_sp - 1)
    send_own(0)

    ids_load.wait()
    logit_load.wait()
    zero = (ids_ref[...] == 0).astype(f32)
    first, second = zero[0:1, :], zero[1:2, :]
    routed = jnp.maximum(first, second)
    logits = logit_ref[...]
    own_logit = jnp.where(first > 0.0, logits[0:1, :], logits[1:2, :])
    other_logit = jnp.where(first > 0.0, logits[1:2, :], logits[0:1, :])
    weight = routed * jax.nn.sigmoid(own_logit - other_logit)
    along = lax.broadcasted_iota(jnp.int32, (tokens, tokens), 0)
    across = lax.broadcasted_iota(jnp.int32, (tokens, tokens), 1)
    before = jnp.where(along <= across, 1.0, 0.0).astype(bf)
    rank = jnp.dot(jnp.broadcast_to(routed, (16, tokens)).astype(bf), before, preferred_element_type=f32)[0:1, :] - 1.0
    chooser = jnp.where(along.astype(f32) == rank, 1.0, 0.0) * routed
    choose_slot[...] = chooser[:slot_rows, :].astype(bf)
    slot_weight[...] = jnp.sum(chooser[:slot_rows, :] * weight, axis=1, keepdims=True)
    choose_tok[...] = jnp.transpose(chooser).astype(bf)
    token_weight[...] = jnp.transpose(jnp.broadcast_to(weight, (tokens, tokens)))

    dout_load.wait()

    def slot_step(step, carry):
        cols = pl.ds(pl.multiple_of(step * tn, tn), tn)
        picked = jnp.dot(choose_slot[...], dout[:, cols], preferred_element_type=f32)
        dcyc[sp, :, cols] = (slot_weight[...] * picked).astype(bf)
        return carry

    lax.fori_loop(0, n_col, slot_step, 0)

    relayed = n_sp == 4
    if relayed:
        near = [sp + 1 - 2 * lax.rem(sp, 2), lax.rem(sp + 2, 4)]
    else:
        near = [lax.rem(sp + off, n_sp) for off in range(1, n_sp)]
    ways = range(len(near))
    half_rows, half_dp = slot_rows // 2, (n_dp - 2) // 2

    def g_send(way):
        return remote(dcyc.at[sp], dcyc.at[sp], gsend.at[way], grecv.at[sp], sp=near[way])

    def b_send(way):
        return remote(dall.at[2:, sp], dall.at[2:, sp], bsend.at[way], brecv.at[sp], sp=near[way])

    def g_half(source, way):
        return dcyc.at[source, way * half_rows:(way + 1) * half_rows]

    def b_half(source, way):
        return dall.at[2 + way * half_dp:2 + (way + 1) * half_dp, source]

    def g_pass(way):
        held = g_half(near[way], way)
        return remote(held, held, fsend.at[way], frecv.at[way], sp=near[1 - way])

    def b_pass(way):
        held = b_half(near[way], way)
        return remote(held, held, fsend.at[2 + way], frecv.at[2 + way], sp=near[1 - way])

    for way in ways:
        g_send(way).start()
    for apart in range(1, chips):
        a_send(apart).start()
    for p in range(1, PIECES):
        make_hidden(p)
        send_own(p)
    late_hid[...] = jnp.zeros_like(late_hid)
    late_cot[...] = jnp.zeros_like(late_cot)

    def r_send(step, off):
        other = lax.rem(sp + off, n_sp)
        cols = pl.ds(pl.multiple_of(step * tn, tn), tn)
        return remote(
            part.at[other, :, cols], rs_ref.at[sp, :, cols],
            rsend.at[step, off], rrecv.at[step, sp], sp=other,
        )

    def half_cols(step, way):
        half = tn // 2
        return pl.ds(pl.multiple_of(step * tn + way * half, half), half)

    def r_hop(step, way, kind):
        cols = half_cols(step, way)
        src = [part.at[near[way], :, cols], part.at[3 - sp, :, cols], rs_ref.at[3, :, cols]][kind]
        return remote(
            src, rs_ref.at[kind, :, cols], rsend.at[step, 2 * kind + way], rrecv.at[step, 2 * kind + way],
            sp=near[1 - way if kind == 2 else way],
        )

    def r_arrived(step, way, kind):
        arrived(rs_ref.at[kind, :, half_cols(step, way)], rrecv.at[step, 2 * kind + way])

    def fold_step(step, carry):
        for way in range(2):
            cols = half_cols(step, way)
            r_arrived(step, way, 1)
            rs_ref[3, :, cols] = (
                part[near[1 - way], :, cols].astype(f32) + rs_ref[1, :, cols].astype(f32)
            ).astype(bf)
            r_hop(step, way, 2).start()
        return carry

    def col_step(step, carry):
        slot = lax.rem(step, 2)

        @pl.when(step + 1 < n_col)
        def _():
            col_load(step + 1, 1 - slot).start()

        col_load(step, slot).wait()
        cols = pl.ds(pl.multiple_of(step * tn, tn), tn)
        product = jnp.dot(hall[dp], wcol[slot], preferred_element_type=f32)
        part[:, :, cols] = product.astype(bf).reshape(n_sp, slot_rows, tn)
        return carry

    lax.fori_loop(0, n_col, col_step, 0)

    def part_sends(kind):
        def step_sends(step, carry):
            if relayed:
                for way in range(2):
                    r_hop(step, way, kind).start()
            else:
                for off in range(1, n_sp):
                    r_send(step, off).start()
            return carry

        lax.fori_loop(0, n_col, step_sends, 0)

    def relay(step, p):
        @pl.when(chip - step >= 0)
        def _():
            index = dp - 2 * step
            h_wait(index, p)

            @pl.when(chip + 1 < chips)
            def _():
                h_right(index, p, step).start()

            h_pair(index, p).start()

        @pl.when(chip + step < chips)
        def _():
            index = dp + 2 * step
            h_wait(index, p)

            @pl.when(chip >= 1)
            def _():
                h_left(index, p, step).start()

            h_pair(index, p).start()

    last = chips - 1
    for rel in range(1, chips):
        arrived(shared.at[rel], arecv.at[rel])
        a_own(rel).start()
        a_mate(rel).start()
    for rel in range(1, chips):
        a_own(rel).wait()
        arrived(dall.at[2 * rel + 1 - core, sp], mate_recv.at[rel])
    for way in ways:
        b_send(way).start()
    for way in ways:
        arrived(dcyc.at[near[way]], grecv.at[near[way]])
        if relayed:
            g_pass(way).start()
    part_sends(1)
    for p in range(PIECES - LATE):
        if last > 1:
            relay(1, p)
    for way in ways:
        arrived(dall.at[2:, near[way]], brecv.at[near[way]])
        if relayed:
            b_pass(way).start()
    if relayed:
        part_sends(0)
    for p in range(PIECES - LATE, PIECES):
        if last > 1:
            relay(1, p)

    if relayed:
        for way in ways:
            arrived(g_half(3 - sp, way), frecv.at[way])

    own_copy = pltpu.make_async_copy(dcyc.at[:, :, block_cols(dp)], dall.at[core], local_sem.at[0])
    mate_copy = remote(
        dcyc.at[:, :, block_cols(partner)], dall.at[core], mate_send.at[0], mate_recv.at[0], dp=partner
    )
    own_copy.start()
    mate_copy.start()

    def row_step(step, carry):
        slot = lax.rem(step, 2)

        @pl.when(step + 1 < n_row)
        def _():
            row_load(step + 1, 1 - slot).start()

        row_load(step, slot).wait()
        cols = pl.ds(pl.multiple_of(step * th, th), th)
        d_hidden = lax.dot_general(
            dcyc[...].reshape(slots, width), wrow[slot], (((1,), (1,)), ((), ())), preferred_element_type=f32
        )
        gate_wide, up_wide = gate[:, cols].astype(f32), up[:, cols].astype(f32)
        sigma = jax.nn.sigmoid(gate_wide)
        ggrad_ref[:, cols] = (d_hidden * up_wide * sigma * (1.0 + gate_wide * (1.0 - sigma))).astype(bf)
        ugrad_ref[:, cols] = (d_hidden * (gate_wide * sigma)).astype(bf)
        return carry

    for p in range(PIECES):
        lax.fori_loop(p * n_row // PIECES, (p + 1) * n_row // PIECES, row_step, 0)
        if last > 2:
            relay(2, p)
        if relayed and p == 1:
            lax.fori_loop(0, n_col, fold_step, 0)

    wide = 256 if block % 256 == 0 else 128

    def cotangents(source, cols):
        rel = lax.rem(source - chip + chips, chips)
        return dall[pl.ds(2 * rel, 2), :, :, cols].reshape(2, slots, -1)

    def down_pass(source, span, initial):
        left = hall[pl.ds(2 * source, 2), :span].reshape(2 * span, hid_width)
        for start in range(0, block, wide):
            cols = slice(start, start + wide)
            product = lax.dot_general(
                left, cotangents(source, cols)[:, :span].reshape(2 * span, wide),
                (((0,), (0,)), ((), ())), preferred_element_type=f32,
            )
            if initial:
                down_ref[:, cols] = product
            else:
                down_ref[:, cols] += product

    own_copy.wait()
    arrived(dall.at[1 - core], mate_recv.at[0])
    for p in range(PIECES):
        h_wait(partner, p)
    down_pass(chip, slots, True)

    wgrad[...] = jnp.zeros_like(wgrad)

    def mix_step(step, carry):
        cols = pl.ds(pl.multiple_of(step * tn, tn), tn)
        total = part[sp, :, cols].astype(f32)
        if relayed:
            for kind in (0, 2):
                for way in range(2):
                    r_arrived(step, way, kind)
                total = total + rs_ref[kind, :, cols].astype(f32)
        else:
            for off in range(1, n_sp):
                other = lax.rem(sp + off, n_sp)
                arrived(rs_ref.at[other, :, cols], rrecv.at[step, other])
                total = total + rs_ref[other, :, cols].astype(f32)
        high = total.astype(bf)
        low = (total - high.astype(f32)).astype(bf)
        choose = choose_tok[:, :slot_rows]
        token_out = jnp.dot(choose, high, preferred_element_type=f32) + jnp.dot(
            choose, low, preferred_element_type=f32
        )
        mixed_ref[:, cols] = (token_weight[:, 0:1] * token_out).astype(bf)
        wgrad[...] += jnp.sum(dout[:, cols].astype(f32) * token_out, axis=1, keepdims=True)
        if relayed:
            for kind in range(3):
                for way in range(2):
                    r_hop(step, way, kind).wait_send()
        else:
            for off in range(1, n_sp):
                r_send(step, off).wait_send()
        return carry

    for step in range(3, last):
        for p in range(PIECES):
            relay(step, p)

    if relayed:
        for way in ways:
            arrived(b_half(3 - sp, way), frecv.at[2 + way])

    def down_step(index, carry):
        source = chip + (lax.div(index, 2) + 1) * (2 * lax.rem(index, 2) - 1)

        @pl.when((source >= 0) & (source < chips))
        def _():
            for p in range(PIECES):
                h_wait(2 * source + 1 - core, p)
            down_pass(source, slots, False)

        return carry

    if last > 1:
        lax.fori_loop(0, 2 * (last - 1), down_step, 0)

    ends = (chip == 0) | (chip == last)
    far = last - chip

    def forward(p):
        @pl.when(ends)
        def _():
            h_wait(2 * far + core, p)
            h_pair(2 * far + core, p).start()

    for p in range(2):
        forward(p)

    lax.fori_loop(0, n_col, mix_step, 0)

    slope = jnp.transpose(jnp.broadcast_to(wgrad[...], (tokens, tokens)))[0:1, :] * weight * (1.0 - weight)
    first_col = jnp.where(first > 0.0, slope, -slope)
    lgrad_ref[0:1, :] = first_col
    lgrad_ref[1:2, :] = -first_col

    mate_copy.wait_send()
    for way in ways:
        g_send(way).wait_send()
        b_send(way).wait_send()
        if relayed:
            g_pass(way).wait_send()
            b_pass(way).wait_send()
    for apart in range(1, chips):
        a_send(apart).wait_send()
        a_mate(apart).wait_send()

    def sent(step, p):
        @pl.when((chip - step >= 0) & (chip + 1 < chips))
        def _():
            h_right(dp, p, step).wait_send()

        @pl.when((chip + step < chips) & (chip >= 1))
        def _():
            h_left(dp, p, step).wait_send()

    for p in range(PIECES):
        for step in range(last):
            sent(step, p)

    for p in range(2, PIECES - LATE):
        forward(p)

    @pl.when(ends)
    def _():
        for p in range(PIECES - LATE):
            h_wait(2 * far + 1 - core, p)
        down_pass(far, early, False)
        late_cot[...] = cotangents(far, slice(None))[:, early:].reshape(2 * late, block)

    for p in range(PIECES - LATE, PIECES):
        forward(p)

    @pl.when(ends)
    def _():
        for p in range(PIECES - LATE, PIECES):
            h_wait(2 * far + 1 - core, p)
        late_hid[...] = hall[pl.ds(2 * far, 2), early:].reshape(2 * late, hid_width)

    for step in range(chips):
        for p in range(PIECES):
            h_send(dp, p, partner, pair_send.at[PIECES * step + p]).wait_send()


def fused(n_dp, n_sp, ids, logits, gate_pre, up_pre, w_down, d_out):
    slots, hid_width = gate_pre.shape
    tokens, width = d_out.shape
    slot_rows = slots // n_sp
    block = width // n_dp
    tn, th = width // 8, min(256, hid_width // 8)
    n_col = width // tn
    chips = n_dp // 2
    late = slots - CUTS[-1 - LATE] * slots // CUTS[-1]
    f32, bf = jnp.float32, jnp.bfloat16
    dma = pltpu.SemaphoreType.DMA
    hbm = pl.BlockSpec(memory_space=pl.ANY)
    vmem = pl.BlockSpec(memory_space=pltpu.VMEM)
    buffers = [
        (ids.shape, ids.dtype), (logits.shape, logits.dtype),
        ((slots, hid_width), bf), ((slots, hid_width), bf), ((tokens, width), bf),
        ((n_dp, slots, hid_width), bf), ((n_dp, n_sp, slot_rows, block), bf),
        ((n_sp, slot_rows, width), bf), ((n_sp, slot_rows, width), bf), ((n_sp, slot_rows, width), bf),
        ((2, hid_width, tn), bf), ((2, th, width), bf),
        ((slot_rows, tokens), bf), ((slot_rows, 1), f32), ((tokens, tokens), bf), ((tokens, tokens), f32),
        ((tokens, 1), f32), ((chips, slot_rows, 2 * block), bf),
    ]
    results = [
        ((tokens, width), bf), ((2, tokens), f32), ((slots, hid_width), bf), ((slots, hid_width), bf),
        ((hid_width, block), f32), ((2 * late, hid_width), bf), ((2 * late, block), bf),
    ]
    kept = sum(math.prod(shape) * jnp.dtype(dtype).itemsize for shape, dtype in results)
    return pl.pallas_call(
        functools.partial(fused_kernel, n_dp, n_sp),
        out_shape=tuple(pltpu.VMEM(shape, dtype) for shape, dtype in results),
        in_specs=[hbm] * 6,
        out_specs=(vmem,) * 7,
        scratch_shapes=[pltpu.VMEM(shape, dtype) for shape, dtype in buffers] + [
            dma((2 * PIECES + 3,)),
            dma((4,)),
            dma((chips,)),
            dma((PIECES * chips,)),
            dma((PIECES * chips,)),
            dma((PIECES * chips,)),
            dma((PIECES * n_dp,)),
            dma((chips,)),
            dma((chips,)),
            dma((n_sp,)),
            dma((n_sp,)),
            dma((n_sp,)),
            dma((n_sp,)),
            dma((n_col, max(n_sp, 6))),
            dma((n_col, max(n_sp, 6))),
            dma((4,)),
            dma((4,)),
            dma((chips,)),
            dma((chips,)),
        ],
        compiler_params=pltpu.CompilerParams(
            collective_id=0, has_side_effects=True, vmem_limit_bytes=62 * 1024 * 1024 - kept
        ),
    )(ids, logits, gate_pre, up_pre, w_down, d_out)


def finish_kernel(
    mixed_ref, slopes_ref, ggrad_ref, ugrad_ref, down_ref, late_hid, late_cot,
    mixed_out, slopes_out, ggrad_out, ugrad_out, down_out, total, sems,
):
    done = [(mixed_ref, mixed_out), (slopes_ref, slopes_out), (ggrad_ref, ggrad_out), (ugrad_ref, ugrad_out)]
    copies = [pltpu.make_async_copy(src, dst, sems.at[i]) for i, (src, dst) in enumerate(done)]
    for copy in copies:
        copy.start()
    span = total.shape[0] // CHUNKS
    for chunk in range(CHUNKS):
        here = slice(chunk * span, (chunk + 1) * span)
        total[here] = down_ref[here] + lax.dot_general(
            late_hid[:, here], late_cot[...], (((0,), (0,)), ((), ())), preferred_element_type=jnp.float32
        )
        copies.append(pltpu.make_async_copy(total.at[here], down_out.at[here], sems.at[len(done) + chunk]))
        copies[-1].start()
    for copy in copies:
        copy.wait()


def finish(*arrays):
    down = arrays[4]
    return pl.pallas_call(
        finish_kernel,
        out_shape=tuple(jax.ShapeDtypeStruct(array.shape, array.dtype) for array in arrays[:5]),
        in_specs=[pl.BlockSpec(memory_space=pltpu.VMEM)] * len(arrays),
        out_specs=(pl.BlockSpec(memory_space=pl.ANY),) * 5,
        scratch_shapes=[pltpu.VMEM(down.shape, down.dtype), pltpu.SemaphoreType.DMA((4 + CHUNKS,))],
        compiler_params=pltpu.CompilerParams(vmem_limit_bytes=16 * 1024 * 1024),
    )(*[pltpu.with_memory_space_constraint(array, pltpu.VMEM) for array in arrays])


def local(n_dp, n_sp, gate_pre, up_pre, w_down, route_logits, expert_ids, d_out):
    mixed, slopes, gate_grads, up_grads, down_grads = finish(*fused(
        n_dp, n_sp, expert_ids.T, route_logits.T, gate_pre, up_pre, w_down, d_out
    ))
    return (mixed, slopes.T, gate_grads, up_grads, down_grads)


def solution(mesh):
    both = P(("dp", "sp"), None)
    return jax.shard_map(
        functools.partial(local, mesh.shape["dp"], mesh.shape["sp"]),
        mesh=mesh,
        in_specs=(P("dp", "sp"), P("dp", "sp"), P("sp", None), both, both, both),
        out_specs=(both, both, P("dp", "sp"), P("dp", "sp"), P("sp", "dp")),
        check_vma=False,
    )
```
